32 devices in a mesh: tm: 16 (over z, y, x), mp: 2 (over core).
Axes of the slice: x: 2, y: 2, z: 4, core: 2. Of those that a mesh axis runs over, the one named last changes fastest.
Arguments:
- filterbank: bfloat16 [4, 16384, 80], P(None, 'tm'), may hold values from -6 to 6
- lengths: int32 [4], replicated, may hold values from 2048 to 4096, as said below
- bank_begin: int32 [4, 1024], P(None, 'tm'), may hold values from 0 to 1023, as said below
- memory_in: bfloat16 [4, 1024, 1024], P(None, 'tm', 'mp'), may hold values from -6 to 6
- w_front: bfloat16 [320, 1024], P(None, 'mp'), may hold values from -0.3125 to 0.3125
- gain_attn: float32 [1024], replicated, may hold values from 0.25 to 1.75
- w_query: bfloat16 [1024, 1024], P(None, 'mp'), may hold values from -0.1875 to 0.1875
- w_key: bfloat16 [1024, 1024], P(None, 'mp'), may hold values from -0.1875 to 0.1875
- w_value: bfloat16 [1024, 1024], P(None, 'mp'), may hold values from -0.1875 to 0.1875
- w_out: bfloat16 [1024, 1024], P('mp'), may hold values from -0.1875 to 0.1875
- gain_ffn: float32 [1024], replicated, may hold values from 0.25 to 1.75
- w_up: bfloat16 [1024, 4096], P(None, 'mp'), may hold values from -0.1875 to 0.1875
- w_down: bfloat16 [4096, 1024], P('mp'), may hold values from -0.09375 to 0.09375
Outputs:
- encoded: bfloat16 [4, 4096, 1024], P(None, 'tm', 'mp')
- memory_out: bfloat16 [4, 1024, 1024], P(None, 'tm', 'mp')
The draws below stay inside these ranges and needn't reach their ends.
Inputs may be any that keep to these rules, and one draw needn't show every extreme that they name: `lengths`: some utterance has all 4096 frames. For segment i: max(0, i - 32) <= bank_begin <= max(0, i - 16); in each utterance some segment has bank_begin = i - 32.
All inputs are finite; a program needn't handle non-finite values.
Results may differ from the reference program's by a relative error of at most 0.012.
Values may be sent and summed in bfloat16 or wider, within the bound.
A program may use at most 128 MiB of HBM per device.

```python
import jax
import jax.numpy as jnp
from jax import lax

D = 1024
HEAD_DIM = 64
FF = 4096
FBANK = 80
STACK = 4
SEG = 4
LC = 32
RC = 4
M = 32
UTT = 4
FRAMES = 4096
SEGMENTS = 1024
N_MP = 2


def draw_lengths(key, part):
    lower_end = FRAMES // 2
    drawn = jax.random.randint(jax.random.fold_in(key, 11), (UTT,), lower_end, FRAMES + 1)
    full_one = jax.random.randint(jax.random.fold_in(key, 12), (), 0, UTT)
    return jnp.where(jnp.arange(UTT) == full_one, FRAMES, drawn).astype(jnp.int32)


def draw_bank_begin(key, part):
    bank_span = jax.random.randint(jax.random.fold_in(key, 21), (UTT, SEGMENTS), M // 2, M + 1)
    chosen = jax.random.randint(jax.random.fold_in(key, 22), (UTT,), M, SEGMENTS)
    seg_index = jnp.arange(SEGMENTS, dtype=jnp.int32)
    bank_span = jnp.where(seg_index[None, :] == chosen[:, None], M, bank_span)
    return jnp.maximum(seg_index[None, :] - bank_span, 0).astype(jnp.int32)


def block_levels(rng, shape, cuts, smallest, top_value):
    def one(axis_at, shards_of):
        draws = jax.random.uniform(jax.random.fold_in(jax.random.fold_in(rng, 6), axis_at), (shards_of,), jnp.float32, smallest / len(cuts), top_value / len(cuts))
        return jnp.repeat(jnp.exp(draws), shape[axis_at] // shards_of).reshape((-1,) + (1,) * (len(shape) - axis_at - 1))

    level = one(*cuts[0])
    for cut in cuts[1:]:
        level = level * one(*cut)
    return level


def centred(rng, extent, scale, bound, split=(), held_as=jnp.bfloat16):
    values = scale * jax.random.normal(rng, extent, jnp.float32)
    if split:
        values = values * block_levels(rng, extent, split, -0.22, 0.18)
    return jnp.clip(values, -bound, bound).astype(held_as)


def setup_inputs(seed: int = 0) -> dict:
    key_of = jax.random.split(jax.random.key(seed), 14)
    filterbank = centred(key_of[0], (UTT, STACK * FRAMES, FBANK), 1.0, 6.0, ((1, 16),))
    lengths = draw_lengths(jax.random.fold_in(key_of[13], 71), 0)
    bank_begin = draw_bank_begin(jax.random.fold_in(key_of[13], 71), 0)
    memory_in = centred(key_of[3], (UTT, SEGMENTS, D), 1.0, 6.0, ((1, 16), (2, 2)))
    w_front = centred(key_of[4], (STACK * FBANK, D), (STACK * FBANK) ** -0.5, 0.3125, ((1, 2),))
    gain_attn = jnp.clip(1.0 + 0.15 * jax.random.normal(key_of[5], (D,), jnp.float32), 0.25, 1.75)
    w_query = centred(key_of[6], (D, D), D ** -0.5, 0.1875, ((1, 2),))
    w_key = centred(key_of[7], (D, D), D ** -0.5, 0.1875, ((1, 2),))
    w_value = centred(key_of[8], (D, D), D ** -0.5, 0.1875, ((1, 2),))
    w_out = centred(key_of[9], (D, D), D ** -0.5, 0.1875, ((0, 2),))
    gain_ffn = jnp.clip(1.0 + 0.15 * jax.random.normal(key_of[10], (D,), jnp.float32), 0.25, 1.75)
    w_up = centred(key_of[11], (D, FF), D ** -0.5, 0.1875, ((1, 2),))
    w_down = centred(key_of[12], (FF, D), FF ** -0.5, 0.09375, ((0, 2),))
    return {"filterbank": filterbank, "lengths": lengths, "bank_begin": bank_begin, "memory_in": memory_in, "w_front": w_front, "gain_attn": gain_attn, "w_query": w_query, "w_key": w_key, "w_value": w_value, "w_out": w_out, "gain_ffn": gain_ffn, "w_up": w_up, "w_down": w_down}


epsilon = 1e-05

def normalize(values, gain):
    center = lax.optimization_barrier(jnp.mean(values, axis=-1, keepdims=True))
    shifted = values - center
    spread = lax.optimization_barrier(jnp.mean(shifted * shifted, axis=-1, keepdims=True))
    return shifted * lax.rsqrt(spread + epsilon) * gain.astype(jnp.float32)

def product(inputs, weight):
    flat_rows = inputs.reshape(-1, inputs.shape[-1])
    result = jnp.dot(flat_rows, weight, preferred_element_type=jnp.float32)
    return result.reshape(inputs.shape[:-1] + (weight.shape[1],))

def grouped_product(inputs, weight):
    group_width = inputs.shape[-1] // N_MP
    running = jnp.zeros(inputs.shape[:-1] + (weight.shape[1],), jnp.float32)
    for group_index in range(N_MP):
        input_part = inputs[..., group_index * group_width:(group_index + 1) * group_width]
        weight_part = weight[group_index * group_width:(group_index + 1) * group_width]
        term_value = lax.optimization_barrier(product(input_part, weight_part).astype(jnp.bfloat16))
        running = running + term_value.astype(jnp.float32)
    return running

def attend_utterance(operands):
    query_rows, key_rows, value_rows, query_sum, key_mem, value_mem, length_one, bank_start = operands
    window = LC + SEG + RC
    head_count = D // HEAD_DIM
    key_padded = jnp.pad(key_rows, ((LC, RC), (0, 0)))
    value_padded = jnp.pad(value_rows, ((LC, RC), (0, 0)))
    bank_keys_padded = jnp.pad(key_mem, ((M, 0), (0, 0)))
    bank_values_padded = jnp.pad(value_mem, ((M, 0), (0, 0)))
    segment_ids = jnp.arange(SEGMENTS, dtype=jnp.int32)

    def one_segment(segment, bank_floor):
        seg_start = segment * SEG
        frame_keys = lax.dynamic_slice_in_dim(key_padded, seg_start, window, 0)
        frame_values = lax.dynamic_slice_in_dim(value_padded, seg_start, window, 0)
        bank_keys = lax.dynamic_slice_in_dim(bank_keys_padded, segment, M, 0)
        bank_values = lax.dynamic_slice_in_dim(bank_values_padded, segment, M, 0)
        row_block = jnp.concatenate([lax.dynamic_slice_in_dim(query_rows, seg_start, SEG, 0), lax.dynamic_slice_in_dim(query_sum, segment, 1, 0)], axis=0)
        all_keys = jnp.concatenate([frame_keys, bank_keys], axis=0)
        all_values = jnp.concatenate([frame_values, bank_values], axis=0)
        frame_pos = seg_start - LC + jnp.arange(window, dtype=jnp.int32)
        frame_ok = (frame_pos >= 0) & (frame_pos < length_one)
        bank_index = segment - M + jnp.arange(M, dtype=jnp.int32)
        bank_ok = (bank_index >= bank_floor) & (bank_index <= segment - 1)
        allowed = jnp.concatenate([frame_ok, bank_ok])
        query_heads = row_block.astype(jnp.float32).reshape(SEG + 1, head_count, HEAD_DIM)
        key_heads = all_keys.astype(jnp.float32).reshape(-1, head_count, HEAD_DIM)
        value_heads = all_values.astype(jnp.float32).reshape(-1, head_count, HEAD_DIM)
        scores = jnp.einsum('qhd,khd->hqk', query_heads, key_heads) * HEAD_DIM ** (-0.5)
        weights = jnp.where(allowed[None, None, :], jnp.exp(scores), 0.0)
        shares = (weights / lax.optimization_barrier(jnp.sum(weights, axis=-1, keepdims=True))).astype(jnp.bfloat16)
        mixture = jnp.einsum('hqk,khd->qhd', shares.astype(jnp.float32), value_heads)
        return mixture.reshape(SEG + 1, D).astype(jnp.bfloat16)
    outputs = jax.vmap(one_segment)(segment_ids, bank_start)
    frame_context = outputs[:, :SEG].reshape(FRAMES, D)
    summary_context = outputs[:, SEG]
    return (frame_context, summary_context)

def reference(filterbank, lengths, bank_begin, memory_in, w_front, gain_attn, w_query, w_key, w_value, w_out, gain_ffn, w_up, w_down):
    stacked = filterbank.reshape(UTT, FRAMES, STACK * FBANK)
    positions = jnp.arange(FRAMES, dtype=jnp.int32)
    valid_frame = positions[None, :] < lengths[:, None]
    front_out = product(stacked, w_front)
    inputs = jnp.where(valid_frame[:, :, None], front_out, 0.0).astype(jnp.bfloat16)
    summary = lax.optimization_barrier(jnp.mean(inputs.astype(jnp.float32).reshape(UTT, SEGMENTS, SEG, D), axis=2))
    normed = normalize(inputs.astype(jnp.float32), gain_attn).astype(jnp.bfloat16)
    normed_sum = normalize(summary, gain_attn).astype(jnp.bfloat16)
    normed_mem = normalize(memory_in.astype(jnp.float32), gain_attn).astype(jnp.bfloat16)
    queries = product(normed, w_query).astype(jnp.bfloat16)
    key_rows = product(normed, w_key).astype(jnp.bfloat16)
    value_rows = product(normed, w_value).astype(jnp.bfloat16)
    query_sum = product(normed_sum, w_query).astype(jnp.bfloat16)
    key_mem = product(normed_mem, w_key).astype(jnp.bfloat16)
    value_mem = product(normed_mem, w_value).astype(jnp.bfloat16)
    frame_context, summary_context = lax.map(attend_utterance, (queries, key_rows, value_rows, query_sum, key_mem, value_mem, lengths, bank_begin))
    attention = grouped_product(frame_context, w_out)
    memory = grouped_product(summary_context, w_out)
    hidden_in = (inputs.astype(jnp.float32) + attention).astype(jnp.bfloat16)
    seg_first = jnp.arange(SEGMENTS, dtype=jnp.int32) * SEG
    valid_seg = seg_first[None, :] < lengths[:, None]
    memory_out = jnp.where(valid_seg[:, :, None], memory, 0.0).astype(jnp.bfloat16)
    normed_ffn = normalize(hidden_in.astype(jnp.float32), gain_ffn).astype(jnp.bfloat16)
    hidden = jax.nn.gelu(product(normed_ffn, w_up)).astype(jnp.bfloat16)
    feed_out = grouped_product(hidden, w_down)
    encoded = jnp.where(valid_frame[:, :, None], hidden_in.astype(jnp.float32) + feed_out, 0.0).astype(jnp.bfloat16)
    return (encoded, memory_out)
```

```python
import functools
import math

import jax
import jax.numpy as jnp
from jax import lax
from jax.experimental import pallas as pl
from jax.experimental.pallas import tpu as pltpu
from jax.sharding import PartitionSpec as P

HEAD_DIM = 64
STACK = 4
SEG = 4
LC = 32
RC = 4
M = 32

TQ = 128
TS = TQ // SEG
TR = TQ + TS
KB = TS + M
KF = 256 - KB
RB = 16
CH = 32

EPS = 1e-05
NEG = -1e30
F32 = jnp.float32
BF16 = jnp.bfloat16
MESH = pl.DeviceIdType.MESH


def dot(a, b):
    return jnp.dot(a, b, preferred_element_type=F32)


def normed_rows(x, gain):
    width = x.shape[-1]
    center = jnp.sum(x, axis=-1, keepdims=True) * (1.0 / width)
    shifted = x - center
    spread = jnp.sum(shifted * shifted, axis=-1, keepdims=True) * (1.0 / width)
    return (shifted * lax.rsqrt(spread + EPS) * gain).astype(BF16)


def gelu(v):
    inner = math.sqrt(2.0 / math.pi) * (v + 0.044715 * (v * v * v))
    return 0.5 * v * (1.0 + jnp.tanh(inner))


def kernel(
    n_tm,
    lengths, bank, gain_a, gain_f, fb_h, mem_h, wf_h, wq_h, wk_h, wv_h, wo_h, wu_h, wd_h,
    enc_h, mo_h,
    fbv, fb32, fbl, fbr, wf, mem, memh, wq, wk, wv, wo, wu, wd,
    inp, nrm, qt, kf, vf, kb, vb, bias, ctx, part, precv, sums, srecv,
    hid, act, feed, frecv, outb, moutb,
    lsem, osem, ssem, rsem, psend, prsem, msend, mrsem, fsend, frsem,
):
    utts, raw, ch = fb_h.shape
    fd = raw // STACK
    sd = fd // SEG
    half = mem_h.shape[2]
    full = 2 * half
    ff = wu_h.shape[1]
    tiles = fd // TQ
    me = lax.axis_index("tm")
    mp = lax.axis_index("mp")
    other = 1 - mp
    nxt = lax.rem(me + 1, n_tm)
    prv = lax.rem(me + n_tm - 1, n_tm)
    partner_id = (me, other)
    next_id = (nxt, mp)
    prev_id = (prv, mp)
    first = me * fd
    seg0 = me * sd

    barrier = pltpu.get_barrier_semaphore()
    for target in (partner_id, next_id, prev_id):
        pl.semaphore_signal(barrier, inc=1, device_id=target, device_id_type=MESH)

    def local(i, src, dst):
        return pltpu.make_async_copy(src, dst, lsem.at[i])

    c_wf = local(0, wf_h, wf.at[mp])
    c_fb = local(1, fb_h, fbv)
    c_mem = local(2, mem_h, mem.at[mp])
    c_q = local(3, wq_h, wq)
    c_k = local(4, wk_h, wk)
    c_v = local(5, wv_h, wv)
    c_o = [local(6 + g, wo_h.at[:, pl.ds(g * half, half)], wo.at[g]) for g in range(2)]
    c_u = local(8, wu_h, wu)
    c_d = [local(9 + g, wd_h.at[:, pl.ds(g * half, half)], wd.at[g]) for g in range(2)]
    for c in (c_wf, c_fb, c_mem, c_q, c_k, c_v, *c_o, c_u, *c_d):
        c.start()

    def remote(i, src, dst, target, send=ssem, recv=rsem):
        return pltpu.make_async_remote_copy(
            src_ref=src, dst_ref=dst, send_sem=send.at[i], recv_sem=recv.at[i],
            device_id=target, device_id_type=MESH,
        )

    pl.semaphore_wait(barrier, 3)
    r_wf = remote(0, wf_h, wf.at[mp], partner_id)
    r_mem = remote(1, mem_h, mem.at[mp], partner_id)
    r_fbl = remote(2, fb_h.at[:, pl.ds(raw - STACK * LC, STACK * LC), :], fbl, next_id)
    r_memh = remote(3, mem_h.at[:, pl.ds(sd - M, M), :], memh.at[mp], next_id)
    r_fbr = remote(4, fb_h.at[:, pl.ds(0, STACK * RC), :], fbr, prev_id)
    r_fwd = remote(5, memh.at[mp], memh.at[mp], partner_id)
    for r in (r_wf, r_mem, r_fbl, r_memh, r_fbr):
        r.start()
    a_wf = remote(0, wf_h, wf.at[other], partner_id)
    a_mem = remote(1, mem_h, mem.at[other], partner_id)
    a_fwd = remote(5, memh.at[mp], memh.at[other], partner_id)

    avg = jnp.where(
        lax.broadcasted_iota(jnp.int32, (sd, fd), 1) // SEG
        == lax.broadcasted_iota(jnp.int32, (sd, fd), 0),
        1.0 / SEG, 0.0,
    ).astype(BF16)
    for u in range(utts):
        tail = kf.shape[1] - (LC + fd + RB)
        kf[u, pl.ds(LC + fd + RB, tail), :] = jnp.zeros((tail, half), BF16)
        vf[u, pl.ds(LC + fd + RB, tail), :] = jnp.zeros((tail, half), BF16)

    c_wf.wait()
    c_fb.wait()
    a_wf.wait_recv()
    c_mem.wait()
    a_mem.wait_recv()
    c_q.wait()
    c_k.wait()
    c_v.wait()

    def front(count, g):
        total = None
        for j in range(STACK):
            x = fb32[pl.ds(j, count, stride=STACK), :][:, :ch].astype(BF16)
            term = dot(x, wf[g, pl.ds(j * ch, ch), :])
            total = term if total is None else total + term
        return total

    def stage_a(u, carry):
        length = lengths[u]
        fb32[:, :ch] = fbv[u].astype(F32)
        ok = first + lax.broadcasted_iota(jnp.int32, (fd, half), 0) < length
        for g in range(2):
            inp[u, :, pl.ds(g * half, half)] = jnp.where(ok, front(fd, g), 0.0).astype(BF16)
        gain = gain_a[...]
        summary = dot(avg, inp[u])
        for r in range(0, sd, CH):
            nrm[pl.ds(r, CH), :] = normed_rows(summary[r : r + CH], gain)
        for r in range(0, fd, CH):
            nrm[pl.ds(sd + r, CH), :] = normed_rows(inp[u, pl.ds(r, CH), :].astype(F32), gain)
        for r in range(0, sd, CH):
            x = jnp.concatenate([mem[g, u, pl.ds(r, CH), :] for g in range(2)], axis=1)
            nrm[pl.ds(sd + fd + r, CH), :] = normed_rows(x.astype(F32), gain)
        q = dot(nrm[pl.ds(0, sd + fd), :], wq[...]).astype(BF16)
        for t in range(tiles):
            qt[u, t, pl.ds(0, TQ), :] = q[sd + t * TQ : sd + (t + 1) * TQ]
            qt[u, t, pl.ds(TQ, TS), :] = q[t * TS : (t + 1) * TS]
        for w, frame, mb in ((wk, kf, kb), (wv, vf, vb)):
            y = dot(nrm[pl.ds(sd, fd + sd), :], w[...]).astype(BF16)
            frame[u, pl.ds(LC, fd), :] = y[:fd]
            mb[u, pl.ds(M, sd), :] = y[fd:]
        return carry

    lax.fori_loop(0, utts, stage_a, 0)

    r_memh.wait_recv()
    r_fwd.start()
    r_fbl.wait_recv()
    r_fbr.wait_recv()
    nl = utts * LC
    nr = utts * RB
    for u in range(utts):
        fb32[pl.ds(u * STACK * LC, STACK * LC), :ch] = fbl[u].astype(F32)
        base = STACK * nl + u * STACK * RB
        fb32[pl.ds(base, STACK * RB), :] = jnp.zeros((STACK * RB, fb32.shape[1]), F32)
        fb32[pl.ds(base, STACK * RC), :ch] = fbr[u].astype(F32)
    row = lax.broadcasted_iota(jnp.int32, (nl + nr, half), 0)
    right = row >= nl
    which = jnp.where(right, (row - nl) // RB, row // LC)
    pos = jnp.where(right, first + fd + (row - nl) % RB, first - LC + row % LC)
    limit = jnp.full(row.shape, lengths[0], jnp.int32)
    for u in range(1, utts):
        limit = jnp.where(which == u, lengths[u], limit)
    halo = [
        jnp.where(pos < limit, front(nl + nr, g), 0.0).astype(BF16) for g in range(2)
    ]
    gain = gain_a[...]
    for r in range(0, nl + nr, CH):
        x = jnp.concatenate([h[r : r + CH] for h in halo], axis=1)
        nrm[pl.ds(r, CH), :] = normed_rows(x.astype(F32), gain)
    a_fwd.wait_recv()
    for u in range(utts):
        x = jnp.concatenate([memh[g, u] for g in range(2)], axis=1)
        nrm[pl.ds(nl + nr + u * M, M), :] = normed_rows(x.astype(F32), gain)
    for w, frame, mb in ((wk, kf, kb), (wv, vf, vb)):
        y = dot(nrm[pl.ds(0, nl + nr + utts * M), :], w[...]).astype(BF16)
        for u in range(utts):
            frame[u, pl.ds(0, LC), :] = y[u * LC : (u + 1) * LC]
            frame[u, pl.ds(LC + fd, RB), :] = y[nl + u * RB : nl + (u + 1) * RB]
            mb[u, pl.ds(0, M), :] = y[nl + nr + u * M : nl + nr + (u + 1) * M]

    for c in c_o:
        c.wait()

    def p_copy(u):
        return remote(u, part.at[u], precv.at[u], partner_id, psend, prsem)

    def m_copy(u):
        return remote(u, sums.at[u, other], srecv.at[u], partner_id, msend, mrsem)

    def f_copy(u):
        return remote(u, feed.at[u, other], frecv.at[u], partner_id, fsend, frsem)

    lane_low = lax.broadcasted_iota(jnp.int32, (TR, 2 * HEAD_DIM), 1) < HEAD_DIM
    factor = HEAD_DIM ** (-0.5) * math.log2(math.e)

    def stage_b(u, carry):
        length = lengths[u]
        for t in range(tiles):
            shape = (TR, KF + KB)
            r = lax.broadcasted_iota(jnp.int32, shape, 0)
            c = lax.broadcasted_iota(jnp.int32, shape, 1)
            seg = t * TS + jnp.where(r < TQ, r // SEG, r - TQ)
            pos = t * TQ - LC + c
            frame_ok = (
                (pos >= seg * SEG - LC) & (pos < (seg + 1) * SEG + RC)
                & (pos + first >= 0) & (pos + first < length)
            )
            rs = lax.broadcasted_iota(jnp.int32, (TR, sd), 0)
            seg_s = t * TS + jnp.where(rs < TQ, rs // SEG, rs - TQ)
            hit = lax.broadcasted_iota(jnp.int32, (TR, sd), 1) == seg_s
            low = jnp.sum(
                jnp.where(hit, (bank[pl.ds(u, 1), :] - seg0).astype(F32), 0.0),
                axis=1, keepdims=True,
            )
            j = t * TS - M + (c - KF)
            bank_ok = (j.astype(F32) >= low) & (j <= seg - 1)
            ok = ((c < KF) & frame_ok) | ((c >= KF) & bank_ok)
            bias[...] = jnp.where(ok, 0.0, NEG)
            for hp in range(half // (2 * HEAD_DIM)):
                cols = pl.ds(hp * 2 * HEAD_DIM, 2 * HEAD_DIM)
                q2 = qt[u, t, :, cols]
                k2 = jnp.concatenate(
                    [kf[u, pl.ds(t * TQ, KF), cols], kb[u, pl.ds(t * TS, KB), cols]], axis=0
                )
                v2 = jnp.concatenate(
                    [vf[u, pl.ds(t * TQ, KF), cols], vb[u, pl.ds(t * TS, KB), cols]], axis=0
                )
                outs = []
                for h in range(2):
                    keep = lane_low if h == 0 else jnp.logical_not(lane_low)
                    qm = jnp.where(keep, q2, jnp.zeros_like(q2))
                    s = lax.dot_general(
                        qm, k2, (((1,), (1,)), ((), ())), preferred_element_type=F32
                    )
                    p = jnp.exp2(s * factor + bias[...])
                    share = 1.0 / jnp.sum(p, axis=1, keepdims=True)
                    outs.append(dot((p * share).astype(BF16), v2))
                ctx[pl.ds(t * TR, TR), cols] = jnp.where(lane_low, outs[0], outs[1]).astype(BF16)
        for g in range(2):
            y = dot(ctx[...], wo[g]).astype(BF16)
            for t in range(tiles):
                part[u, g, pl.ds(t * TQ, TQ), :] = y[t * TR : t * TR + TQ]
                sums[u, g, pl.ds(t * TS, TS), :] = y[t * TR + TQ : (t + 1) * TR]
        p_copy(u).start()
        m_copy(u).start()
        return carry

    lax.fori_loop(0, utts, stage_b, 0)

    c_u.wait()
    for c in c_d:
        c.wait()

    def finish(u):
        f_copy(u).wait_recv()
        ok = first + lax.broadcasted_iota(jnp.int32, (fd, half), 0) < lengths[u]
        total = feed[u, mp].astype(F32) + frecv[u].astype(F32)
        total = hid[u, mp].astype(F32) + total
        outb[u] = jnp.where(ok, total, 0.0).astype(BF16)
        pltpu.make_async_copy(outb.at[u], enc_h.at[u], osem.at[u]).start()

    def stage_c(u, carry):
        p_copy(u).wait_recv()
        gain = gain_f[...]
        for r in range(0, fd, CH):
            xs = []
            for g in range(2):
                rows = pl.ds(r, CH)
                att = part[u, g, rows, :].astype(F32) + precv[u, g, rows, :].astype(F32)
                x = (inp[u, rows, pl.ds(g * half, half)].astype(F32) + att).astype(BF16)
                hid[u, g, rows, :] = x
                xs.append(x.astype(F32))
            nrm[pl.ds(r, CH), :] = normed_rows(jnp.concatenate(xs, axis=1), gain)
        step = 512
        for k in range(0, ff, step):
            up = dot(nrm[pl.ds(0, fd), :], wu[:, pl.ds(k, step)])
            act[:, pl.ds(k, step)] = gelu(up).astype(BF16)
        feed[u, other] = dot(act[...], wd[other]).astype(BF16)
        f_copy(u).start()
        feed[u, mp] = dot(act[...], wd[mp]).astype(BF16)

        m_copy(u).wait_recv()
        seg_ok = (seg0 + lax.broadcasted_iota(jnp.int32, (sd, half), 0)) * SEG < lengths[u]
        both = sums[u, mp].astype(F32) + srecv[u].astype(F32)
        moutb[u] = jnp.where(seg_ok, both, 0.0).astype(BF16)
        pltpu.make_async_copy(moutb.at[u], mo_h.at[u], osem.at[utts + u]).start()

        @pl.when(u > 0)
        def _():
            finish(u - 1)

        return carry

    lax.fori_loop(0, utts, stage_c, 0)
    finish(utts - 1)

    for r in (r_wf, r_mem, r_fbl, r_memh, r_fbr, r_fwd):
        r.wait_send()

    def drain(u, carry):
        p_copy(u).wait_send()
        m_copy(u).wait_send()
        f_copy(u).wait_send()
        pltpu.make_async_copy(outb.at[u], enc_h.at[u], osem.at[u]).wait()
        pltpu.make_async_copy(moutb.at[u], mo_h.at[u], osem.at[utts + u]).wait()
        return carry

    lax.fori_loop(0, utts, drain, 0)


def body(n_tm, filterbank, lengths, bank_begin, memory_in, w_front, gain_attn, w_query, w_key,
         w_value, w_out, gain_ffn, w_up, w_down):
    utts, raw, ch = filterbank.shape
    fd = raw // STACK
    sd = fd // SEG
    half = w_query.shape[1]
    full = w_query.shape[0]
    ff = w_up.shape[1]
    tiles = fd // TQ
    kf_rows = (tiles - 1) * TQ + KF
    any_spec = pl.BlockSpec(memory_space=pl.ANY)
    vmem_spec = pl.BlockSpec(memory_space=pltpu.VMEM)
    smem_spec = pl.BlockSpec(memory_space=pltpu.SMEM)
    dma = pltpu.SemaphoreType.DMA
    vm = pltpu.VMEM
    scratch = [
        vm((utts, raw, ch), BF16),
        vm((raw, 128), F32),
        vm((utts, STACK * LC, ch), BF16),
        vm((utts, STACK * RC, ch), BF16),
        vm((2,) + w_front.shape, BF16),
        vm((2, utts, sd, half), BF16),
        vm((2, utts, M, half), BF16),
        vm((full, half), BF16),
        vm((full, half), BF16),
        vm((full, half), BF16),
        vm((2, half, half), BF16),
        vm((full, ff), BF16),
        vm((2, ff, half), BF16),
        vm((utts, fd, full), BF16),
        vm((fd + 2 * sd, full), BF16),
        vm((utts, tiles, TR, half), BF16),
        vm((utts, kf_rows, half), BF16),
        vm((utts, kf_rows, half), BF16),
        vm((utts, M + sd, half), BF16),
        vm((utts, M + sd, half), BF16),
        vm((TR, KF + KB), F32),
        vm((fd + sd, half), BF16),
        vm((utts, 2, fd, half), BF16),
        vm((utts, 2, fd, half), BF16),
        vm((utts, 2, sd, half), BF16),
        vm((utts, sd, half), BF16),
        vm((utts, 2, fd, half), BF16),
        vm((fd, ff), BF16),
        vm((utts, 2, fd, half), BF16),
        vm((utts, fd, half), BF16),
        vm((utts, fd, half), BF16),
        vm((utts, sd, half), BF16),
        dma((11,)), dma((2 * utts,)), dma((6,)), dma((6,)),
        dma((utts,)), dma((utts,)), dma((utts,)), dma((utts,)), dma((utts,)), dma((utts,)),
    ]
    return pl.pallas_call(
        functools.partial(kernel, n_tm),
        out_shape=(
            jax.ShapeDtypeStruct((utts, fd, half), BF16),
            jax.ShapeDtypeStruct((utts, sd, half), BF16),
        ),
        in_specs=[smem_spec, vmem_spec, vmem_spec, vmem_spec] + [any_spec] * 9,
        out_specs=(any_spec, any_spec),
        scratch_shapes=scratch,
        compiler_params=pltpu.CompilerParams(
            collective_id=0, has_side_effects=True, vmem_limit_bytes=60 * 1024 * 1024
        ),
    )(
        lengths, bank_begin, gain_attn.reshape(1, full), gain_ffn.reshape(1, full),
        filterbank, memory_in, w_front, w_query, w_key, w_value, w_out, w_up, w_down,
    )


def solution(mesh):
    in_specs = (
        P(None, "tm", None),
        P(),
        P(None, "tm"),
        P(None, "tm", "mp"),
        P(None, "mp"),
        P(),
        P(None, "mp"),
        P(None, "mp"),
        P(None, "mp"),
        P("mp", None),
        P(),
        P(None, "mp"),
        P("mp", None),
    )
    out_specs = (P(None, "tm", "mp"), P(None, "tm", "mp"))
    return jax.shard_map(
        functools.partial(body, mesh.shape["tm"]),
        mesh=mesh, in_specs=in_specs, out_specs=out_specs, check_vma=False,
    )
```

```python
import functools
import math

import jax
import jax.numpy as jnp
from jax import lax
from jax.experimental import pallas as pl
from jax.experimental.pallas import tpu as pltpu
from jax.sharding import PartitionSpec as P

HEAD_DIM = 64
STACK = 4
SEG = 4
LC = 32
RC = 4
M = 32

TQ = 128
TS = TQ // SEG
TR = TQ + TS
KB = TS + M
KF = 256 - KB
RB = 16
CH = 32

EPS = 1e-05
NEG = -1e30
F32 = jnp.float32
BF16 = jnp.bfloat16
MESH = pl.DeviceIdType.MESH


def dot(a, b):
    return jnp.dot(a, b, preferred_element_type=F32)


def normed_rows(x, gain):
    width = x.shape[-1]
    center = jnp.sum(x, axis=-1, keepdims=True) * (1.0 / width)
    shifted = x - center
    spread = jnp.sum(shifted * shifted, axis=-1, keepdims=True) * (1.0 / width)
    return (shifted * lax.rsqrt(spread + EPS) * gain).astype(BF16)


def gelu(v):
    c = math.sqrt(2.0 / math.pi)
    half_v = 0.5 * v
    return half_v + half_v * jnp.tanh(v * (c + (0.044715 * c) * (v * v)))


def kernel(
    n_tm,
    lengths, bank, gain_a, gain_f, fb_h, mem_h, wf_h, wq_h, wk_h, wv_h, wo_h, wu_h, wd_h,
    outb, moutb,
    fbv, fb32, fbl, fbr, wf, mem, memh, wq, wk, wv, wo, wu, wd,
    inp, nrm, stk, smry, qt, kf, vf, kb, vb, bias, ctx, part, precv, sums, srecv,
    hid, act, feed, frecv,
    lsem, ssem, rsem, psend, prsem, msend, mrsem, fsend, frsem,
):
    utts, ch, raw = fb_h.shape
    fd = raw // STACK
    sd = fd // SEG
    half = mem_h.shape[2]
    full = 2 * half
    ff = wu_h.shape[1]
    tiles = fd // TQ
    me = lax.axis_index("tm")
    mp = lax.axis_index("mp")
    other = 1 - mp
    nxt = lax.rem(me + 1, n_tm)
    prv = lax.rem(me + n_tm - 1, n_tm)
    partner_id = (me, other)
    next_id = (nxt, mp)
    prev_id = (prv, mp)
    first = me * fd
    seg0 = me * sd

    barrier = pltpu.get_barrier_semaphore()
    for target in (partner_id, next_id, prev_id):
        pl.semaphore_signal(barrier, inc=1, device_id=target, device_id_type=MESH)

    def local(i, src, dst):
        return pltpu.make_async_copy(src, dst, lsem.at[i])

    c_wf = local(0, wf_h, wf.at[mp])
    c_fb = local(1, fb_h, fbv)
    c_mem = local(2, mem_h, mem.at[mp])
    c_q = local(3, wq_h, wq)
    c_k = local(4, wk_h, wk)
    c_v = local(5, wv_h, wv)
    c_o = [local(6 + g, wo_h.at[:, pl.ds(g * half, half)], wo.at[g]) for g in range(2)]
    c_u = local(8, wu_h, wu)
    c_d = [local(9 + g, wd_h.at[:, pl.ds(g * half, half)], wd.at[g]) for g in range(2)]
    for c in (c_wf, c_fb, c_mem, c_q, c_k, c_v, *c_o, c_u, *c_d):
        c.start()

    def remote(i, src, dst, target, send=ssem, recv=rsem):
        return pltpu.make_async_remote_copy(
            src_ref=src, dst_ref=dst, send_sem=send.at[i], recv_sem=recv.at[i],
            device_id=target, device_id_type=MESH,
        )

    pl.semaphore_wait(barrier, 3)
    r_wf = remote(0, wf_h, wf.at[mp], partner_id)
    r_mem = remote(1, mem_h, mem.at[mp], partner_id)
    r_fbl = remote(2, fb_h.at[:, :, pl.ds(raw - STACK * LC, STACK * LC)], fbl, next_id)
    r_memh = remote(3, mem_h.at[:, pl.ds(sd - M, M), :], memh.at[mp], next_id)
    r_fbr = remote(4, fb_h.at[:, :, pl.ds(0, STACK * LC)], fbr, prev_id)
    r_fwd = remote(5, memh.at[mp], memh.at[mp], partner_id)
    for r in (r_wf, r_mem, r_fbl, r_memh, r_fbr):
        r.start()
    a_wf = remote(0, wf_h, wf.at[other], partner_id)
    a_mem = remote(1, mem_h, mem.at[other], partner_id)
    a_fwd = remote(5, memh.at[mp], memh.at[other], partner_id)

    avg = jnp.where(
        lax.broadcasted_iota(jnp.int32, (sd, fd), 1) // SEG
        == lax.broadcasted_iota(jnp.int32, (sd, fd), 0),
        1.0 / SEG, 0.0,
    ).astype(BF16)
    for u in range(utts):
        tail = kf.shape[1] - (LC + fd + RB)
        kf[u, pl.ds(LC + fd + RB, tail), :] = jnp.zeros((tail, half), BF16)
        vf[u, pl.ds(LC + fd + RB, tail), :] = jnp.zeros((tail, half), BF16)

    c_wf.wait()
    c_fb.wait()
    a_wf.wait_recv()
    c_mem.wait()
    a_mem.wait_recv()
    c_q.wait()
    c_k.wait()
    c_v.wait()

    def stacked(count):
        parts = [fb32[pl.ds(j, count, stride=STACK), :][:, :ch] for j in range(STACK)]
        return jnp.concatenate(parts, axis=1).astype(BF16)

    factor = HEAD_DIM ** (-0.5) * math.log2(math.e)

    def front(u):
        fb32[:, :ch] = fbv[u].astype(F32).T
        stk[...] = stacked(fd)
        ok = first + lax.broadcasted_iota(jnp.int32, (fd, half), 0) < lengths[u]
        for g in range(2):
            inp[u, :, pl.ds(g * half, half)] = jnp.where(ok, dot(stk[...], wf[g]), 0.0).astype(BF16)
        smry[...] = dot(avg, inp[u])

    def norm_tasks(u):
        dst = nrm
        gain = gain_a[...]

        def of_summary(r):
            dst[pl.ds(r, CH), :] = normed_rows(smry[pl.ds(r, CH), :], gain)

        def of_frames(r):
            dst[pl.ds(sd + r, CH), :] = normed_rows(inp[u, pl.ds(r, CH), :].astype(F32), gain)

        def of_memory(r):
            x = jnp.concatenate([mem[g, u, pl.ds(r, CH), :] for g in range(2)], axis=1)
            dst[pl.ds(sd + fd + r, CH), :] = normed_rows(x.astype(F32), gain)

        return (
            [functools.partial(of_summary, r) for r in range(0, sd, CH)]
            + [functools.partial(of_frames, r) for r in range(0, fd, CH)]
            + [functools.partial(of_memory, r) for r in range(0, sd, CH)]
        )

    def make_bias(u, t):
        length = lengths[u]
        shape = (TR, KF + KB)
        r = lax.broadcasted_iota(jnp.int32, shape, 0)
        c = lax.broadcasted_iota(jnp.int32, shape, 1)
        seg = t * TS + jnp.where(r < TQ, r // SEG, r - TQ)
        pos = t * TQ - LC + c
        frame_ok = (
            (pos >= seg * SEG - LC) & (pos < (seg + 1) * SEG + RC)
            & (pos + first >= 0) & (pos + first < length)
        )
        rs = lax.broadcasted_iota(jnp.int32, (TR, sd), 0)
        seg_s = t * TS + jnp.where(rs < TQ, rs // SEG, rs - TQ)
        hit = lax.broadcasted_iota(jnp.int32, (TR, sd), 1) == seg_s
        low = jnp.sum(
            jnp.where(hit, (bank[pl.ds(u, 1), :] - seg0).astype(F32), 0.0),
            axis=1, keepdims=True,
        )
        j = t * TS - M + (c - KF)
        bank_ok = (j.astype(F32) >= low) & (j <= seg - 1)
        ok = ((c < KF) & frame_ok) | ((c >= KF) & bank_ok)
        bias[u, t] = jnp.where(ok, 0.0, NEG)

    def spread_over(tasks, pieces):
        done = 0
        for i, piece in enumerate(pieces):
            upto = len(tasks) * (i + 1) // len(pieces)
            for task in tasks[done:upto]:
                task()
            done = upto
            piece()

    def qkv_pieces(u):
        src = nrm
        wide = half // 2

        def query(n):
            q = dot(src[pl.ds(0, sd + fd), :], wq[:, pl.ds(n, wide)]).astype(BF16)
            for t in range(tiles):
                qt[u, t, pl.ds(0, TQ), pl.ds(n, wide)] = q[sd + t * TQ : sd + (t + 1) * TQ]
                qt[u, t, pl.ds(TQ, TS), pl.ds(n, wide)] = q[t * TS : (t + 1) * TS]

        def key_value(w, frame, mb, n):
            y = dot(src[pl.ds(sd, fd + sd), :], w[:, pl.ds(n, wide)]).astype(BF16)
            frame[u, pl.ds(LC, fd), pl.ds(n, wide)] = y[:fd]
            mb[u, pl.ds(M, sd), pl.ds(n, wide)] = y[fd:]

        cuts = range(0, half, wide)
        return (
            [functools.partial(query, n) for n in cuts]
            + [functools.partial(key_value, wk, kf, kb, n) for n in cuts]
            + [functools.partial(key_value, wv, vf, vb, n) for n in cuts]
        )

    def stage_a(u, carry):
        front(u)
        for task in norm_tasks(u):
            task()
        spread_over([functools.partial(make_bias, u, t) for t in range(tiles)], qkv_pieces(u))
        return carry

    lax.fori_loop(0, utts, stage_a, 0)

    r_memh.wait_recv()
    r_fwd.start()
    r_fbl.wait_recv()
    r_fbr.wait_recv()
    nl = utts * LC
    nr = utts * RB
    for u in range(utts):
        fb32[pl.ds(u * STACK * LC, STACK * LC), :ch] = fbl[u].astype(F32).T
        base = STACK * nl + u * STACK * RB
        fb32[pl.ds(base, STACK * RB), :ch] = fbr[u].astype(F32).T[: STACK * RB]
    row = lax.broadcasted_iota(jnp.int32, (nl + nr, half), 0)
    right = row >= nl
    which = jnp.where(right, (row - nl) // RB, row // LC)
    pos = jnp.where(right, first + fd + (row - nl) % RB, first - LC + row % LC)
    limit = jnp.full(row.shape, lengths[0], jnp.int32)
    for u in range(1, utts):
        limit = jnp.where(which == u, lengths[u], limit)
    stk[pl.ds(0, nl + nr), :] = stacked(nl + nr)
    halo = [
        jnp.where(pos < limit, dot(stk[pl.ds(0, nl + nr), :], wf[g]), 0.0).astype(BF16)
        for g in range(2)
    ]
    gain = gain_a[...]
    for r in range(0, nl + nr, CH):
        x = jnp.concatenate([h[r : r + CH] for h in halo], axis=1)
        nrm[pl.ds(r, CH), :] = normed_rows(x.astype(F32), gain)
    a_fwd.wait_recv()
    for u in range(utts):
        x = jnp.concatenate([memh[g, u] for g in range(2)], axis=1)
        nrm[pl.ds(nl + nr + u * M, M), :] = normed_rows(x.astype(F32), gain)
    for w, frame, mb in ((wk, kf, kb), (wv, vf, vb)):
        y = dot(nrm[pl.ds(0, nl + nr + utts * M), :], w[...]).astype(BF16)
        for u in range(utts):
            frame[u, pl.ds(0, LC), :] = y[u * LC : (u + 1) * LC]
            frame[u, pl.ds(LC + fd, RB), :] = y[nl + u * RB : nl + (u + 1) * RB]
            mb[u, pl.ds(0, M), :] = y[nl + nr + u * M : nl + nr + (u + 1) * M]

    for c in c_o:
        c.wait()

    def p_copy(u):
        return remote(u, part.at[u], precv.at[u], partner_id, psend, prsem)

    def m_copy(u):
        return remote(u, sums.at[u, other], srecv.at[u], partner_id, msend, mrsem)

    def f_copy(u):
        return remote(u, feed.at[u, other], frecv.at[u], partner_id, fsend, frsem)

    lane_low = lax.broadcasted_iota(jnp.int32, (TR, 2 * HEAD_DIM), 1) < HEAD_DIM
    def stage_b(u, carry):
        for t in range(tiles):
            for hp in range(half // (2 * HEAD_DIM)):
                cols = pl.ds(hp * 2 * HEAD_DIM, 2 * HEAD_DIM)
                q2 = qt[u, t, :, cols]
                k2 = jnp.concatenate(
                    [kf[u, pl.ds(t * TQ, KF), cols], kb[u, pl.ds(t * TS, KB), cols]], axis=0
                )
                v2 = jnp.concatenate(
                    [vf[u, pl.ds(t * TQ, KF), cols], vb[u, pl.ds(t * TS, KB), cols]], axis=0
                )
                outs = []
                for h in range(2):
                    keep = lane_low if h == 0 else jnp.logical_not(lane_low)
                    qm = jnp.where(keep, q2, jnp.zeros_like(q2))
                    s = lax.dot_general(
                        qm, k2, (((1,), (1,)), ((), ())), preferred_element_type=F32
                    )
                    p = jnp.exp2(s * factor + bias[u, t])
                    share = 1.0 / jnp.sum(p, axis=1, keepdims=True)
                    outs.append(dot((p * share).astype(BF16), v2))
                ctx[pl.ds(t * TR, TR), cols] = jnp.where(lane_low, outs[0], outs[1]).astype(BF16)
        for g in range(2):
            y = dot(ctx[...], wo[g]).astype(BF16)
            for t in range(tiles):
                part[u, g, pl.ds(t * TQ, TQ), :] = y[t * TR : t * TR + TQ]
                sums[u, g, pl.ds(t * TS, TS), :] = y[t * TR + TQ : (t + 1) * TR]
        p_copy(u).start()
        m_copy(u).start()
        return carry

    lax.fori_loop(0, utts, stage_b, 0)

    c_u.wait()
    for c in c_d:
        c.wait()

    def finish_tasks(u):
        def part_of(r):
            rows = pl.ds(r, CH)
            ok = first + r + lax.broadcasted_iota(jnp.int32, (CH, half), 0) < lengths[u]
            total = hid[u, mp, rows, :] + (feed[u, mp, rows, :] + frecv[u, rows, :])
            outb[u, rows, :] = jnp.where(ok, total, jnp.zeros_like(total))

        return [functools.partial(part_of, r) for r in range(0, fd, CH)]

    def summary_out(u):
        seg_ok = (seg0 + lax.broadcasted_iota(jnp.int32, (sd, half), 0)) * SEG < lengths[u]
        both = sums[u, mp].astype(F32) + srecv[u].astype(F32)
        moutb[u] = jnp.where(seg_ok, both, 0.0).astype(BF16)

    def hidden_tasks(u):
        dst = nrm
        gain = gain_f[...]

        def part_of(r):
            xs = []
            rows = pl.ds(r, CH)
            for g in range(2):
                att = part[u, g, rows, :] + precv[u, g, rows, :]
                x = inp[u, rows, pl.ds(g * half, half)] + att
                hid[u, g, rows, :] = x
                xs.append(x.astype(F32))
            dst[rows, :] = normed_rows(jnp.concatenate(xs, axis=1), gain)

        return [functools.partial(part_of, r) for r in range(0, fd, CH)]

    step = 512

    def finish(u):
        f_copy(u).wait_recv()
        for task in finish_tasks(u):
            task()

    def stage_c(u, carry):
        p_copy(u).wait_recv()
        for task in hidden_tasks(u):
            task()
        for k in range(0, ff, step):
            up = dot(nrm[pl.ds(0, fd), :], wu[:, pl.ds(k, step)])
            act[:, pl.ds(k, step)] = gelu(up.astype(BF16))
        feed[u, other] = dot(act[...], wd[other]).astype(BF16)
        f_copy(u).start()
        m_copy(u).wait_recv()
        summary_out(u)
        feed[u, mp] = dot(act[...], wd[mp]).astype(BF16)

        @pl.when(u > 0)
        def _():
            finish(u - 1)

        return carry

    lax.fori_loop(0, utts, stage_c, 0)
    finish(utts - 1)

    for r in (r_wf, r_mem, r_fbl, r_memh, r_fbr, r_fwd):
        r.wait_send()

    def drain(u, carry):
        p_copy(u).wait_send()
        m_copy(u).wait_send()
        f_copy(u).wait_send()
        return carry

    lax.fori_loop(0, utts, drain, 0)


def body(n_tm, filterbank, lengths, bank_begin, memory_in, w_front, gain_attn, w_query, w_key,
         w_value, w_out, gain_ffn, w_up, w_down):
    utts, raw, ch = filterbank.shape
    fd = raw // STACK
    sd = fd // SEG
    half = w_query.shape[1]
    full = w_query.shape[0]
    ff = w_up.shape[1]
    tiles = fd // TQ
    kf_rows = (tiles - 1) * TQ + KF
    any_spec = pl.BlockSpec(memory_space=pl.ANY)
    vmem_spec = pl.BlockSpec(memory_space=pltpu.VMEM)
    smem_spec = pl.BlockSpec(memory_space=pltpu.SMEM)
    dma = pltpu.SemaphoreType.DMA
    vm = pltpu.VMEM
    scratch = [
        vm((utts, ch, raw), BF16),
        vm((raw, 128), F32),
        vm((utts, ch, STACK * LC), BF16),
        vm((utts, ch, STACK * LC), BF16),
        vm((2,) + w_front.shape, BF16),
        vm((2, utts, sd, half), BF16),
        vm((2, utts, M, half), BF16),
        vm((full, half), BF16),
        vm((full, half), BF16),
        vm((full, half), BF16),
        vm((2, half, half), BF16),
        vm((full, ff), BF16),
        vm((2, ff, half), BF16),
        vm((utts, fd, full), BF16),
        vm((fd + 2 * sd, full), BF16),
        vm((fd, STACK * ch), BF16),
        vm((sd, full), F32),
        vm((utts, tiles, TR, half), BF16),
        vm((utts, kf_rows, half), BF16),
        vm((utts, kf_rows, half), BF16),
        vm((utts, M + sd, half), BF16),
        vm((utts, M + sd, half), BF16),
        vm((utts, tiles, TR, KF + KB), F32),
        vm((fd + sd, half), BF16),
        vm((utts, 2, fd, half), BF16),
        vm((utts, 2, fd, half), BF16),
        vm((utts, 2, sd, half), BF16),
        vm((utts, sd, half), BF16),
        vm((utts, 2, fd, half), BF16),
        vm((fd, ff), BF16),
        vm((utts, 2, fd, half), BF16),
        vm((utts, fd, half), BF16),
        dma((11,)), dma((6,)), dma((6,)),
        dma((utts,)), dma((utts,)), dma((utts,)), dma((utts,)), dma((utts,)), dma((utts,)),
    ]
    return pl.pallas_call(
        functools.partial(kernel, n_tm),
        out_shape=(
            pltpu.VMEM((utts, fd, half), BF16),
            pltpu.VMEM((utts, sd, half), BF16),
        ),
        in_specs=[smem_spec, vmem_spec, vmem_spec, vmem_spec] + [any_spec] * 9,
        out_specs=(vmem_spec, vmem_spec),
        scratch_shapes=scratch,
        compiler_params=pltpu.CompilerParams(
            collective_id=0, has_side_effects=True, vmem_limit_bytes=60 * 1024 * 1024
        ),
    )(
        lengths, bank_begin, gain_attn.reshape(1, full), gain_ffn.reshape(1, full),
        jnp.swapaxes(filterbank, 1, 2), memory_in, w_front, w_query, w_key, w_value, w_out, w_up, w_down,
    )


def solution(mesh):
    in_specs = (
        P(None, "tm", None),
        P(),
        P(None, "tm"),
        P(None, "tm", "mp"),
        P(None, "mp"),
        P(),
        P(None, "mp"),
        P(None, "mp"),
        P(None, "mp"),
        P("mp", None),
        P(),
        P(None, "mp"),
        P("mp", None),
    )
    out_specs = (P(None, "tm", "mp"), P(None, "tm", "mp"))
    return jax.shard_map(
        functools.partial(body, mesh.shape["tm"]),
        mesh=mesh, in_specs=in_specs, out_specs=out_specs, check_vma=False,
    )
```
